256 devices in a mesh: dom: 64 (over x, z, core), slab: 4 (over y).
Axes of the slice: x: 4, y: 4, z: 8, core: 2. Of those that a mesh axis runs over, the one named last changes fastest.
Arguments:
- logperm: float32 [256, 16, 64, 128], P('dom', 'slab'), may hold values from -4.2 to 4.2
- source: float32 [16, 64, 128], P('slab'), may hold values from -6 to 6
- observed: float32 [16, 64, 128], P('slab'), may hold values from -1.2 to 1.2
- brownian: float32 [256, 256], replicated, may hold values from -6 to 6
Outputs:
- particles_next: float32 [256, 16, 64, 128], P('dom', 'slab')
The draws below stay inside these ranges and needn't reach their ends.
All inputs are finite; a program needn't handle non-finite values.
Results may differ from the reference program's by a relative error of at most 0.0003.
Values sent between devices are 32-bit elements; how exact they have to be, the bound alone decides.
No kernel may reach another device: no remote copies, remote signals or barrier semaphores. Data moves between devices by JAX's collectives and lax.ppermute only.
A program may use at most 64 MiB of HBM per device.

```python
import math
import jax
import jax.numpy as jnp
from jax import lax

PART_DEV = 4
NY = 64
NZ = 128
SWEEPS = 8
J = 256
NXG = 16
CELLS = 131072


def block_scale(rng, shape, shards, least, high):
    gain = 1.0
    for axis_at, parts in shards:
        heights = jax.random.uniform(jax.random.fold_in(jax.random.fold_in(rng, 6), axis_at), (parts,), jnp.float32, least / len(shards), high / len(shards))
        gain = gain * jnp.repeat(jnp.exp(heights), shape[axis_at] // parts).reshape((-1,) + (1,) * (len(shape) - 1 - axis_at))
    return gain


def normal_values(stream_key, shape, scale, limit, split=(), held_as=jnp.bfloat16):
    array = jax.random.normal(stream_key, shape, jnp.float32) * scale
    if len(split) > 0:
        array = block_scale(stream_key, shape, split, -0.22, 0.18) * array
    return jnp.clip(array, min=-limit, max=limit).astype(held_as)


def setup_inputs(seed: int = 0) -> dict:
    splits = jax.random.split(jax.random.key(seed), 5)
    return {
        "logperm": normal_values(splits[0], (J, NXG, NY, NZ), 0.7, 4.2, ((0, 64), (1, 4)), jnp.float32),
        "source": normal_values(splits[1], (NXG, NY, NZ), 1.0, 6.0, ((0, 4),), jnp.float32),
        "observed": normal_values(splits[2], (NXG, NY, NZ), 0.2, 1.2, ((0, 4),), jnp.float32),
        "brownian": normal_values(splits[3], (J, J), 1.0, 6.0, (), jnp.float32),
    }


misfit_weight = 1000.0

def neighbor_sum(core, below, above, fill):
    pad_y = jnp.pad(core, ((0, 0), (0, 0), (1, 1), (0, 0)), constant_values=fill)
    pad_z = jnp.pad(core, ((0, 0), (0, 0), (0, 0), (1, 1)), constant_values=fill)
    return below + above + pad_y[:, :, :-2] + pad_y[:, :, 2:] + pad_z[..., :-2] + pad_z[..., 2:]

def grad_field(e_core, e_below, e_above, p_core, p_below, p_above, q_core, q_below, q_above):
    summed = e_below * (p_core - p_below) * (q_core - q_below) + e_above * (p_core - p_above) * (q_core - q_above)
    for dimension in (2, 3):
        padding = [(0, 0), (0, 0), (0, 0), (0, 0)]
        padding[dimension] = (1, 1)
        e_pad = jnp.pad(e_core, padding, constant_values=1.0)
        p_pad = jnp.pad(p_core, padding)
        q_pad = jnp.pad(q_core, padding)
        extent = e_core.shape[dimension]
        for offset in (0, 2):
            e_near = lax.slice_in_dim(e_pad, offset, offset + extent, axis=dimension)
            p_near = lax.slice_in_dim(p_pad, offset, offset + extent, axis=dimension)
            q_near = lax.slice_in_dim(q_pad, offset, offset + extent, axis=dimension)
            summed = summed + e_near * (p_core - p_near) * (q_core - q_near)
    return -0.5 * e_core * summed

def field_gradient(block, source, observed):
    e_core = jnp.exp(0.5 * block)
    e_pad = jnp.pad(e_core, ((0, 0), (1, 1), (0, 0), (0, 0)), constant_values=1.0)
    inverse = 1.0 / neighbor_sum(e_core, e_pad[:, :-2], e_pad[:, 2:], 1.0)

    def relax(rhs):
        value = inverse * rhs
        for sweep_index in range(SWEEPS - 1):
            padded = jnp.pad(value, ((0, 0), (1, 1), (0, 0), (0, 0)))
            value = inverse * (rhs + e_core * neighbor_sum(value, padded[:, :-2], padded[:, 2:], 0.0))
        return value / e_core
    pressure = relax(source)
    misfit = misfit_weight * (pressure - observed)
    adjoint = relax(misfit)
    p_pad = jnp.pad(pressure, ((0, 0), (1, 1), (0, 0), (0, 0)))
    q_pad = jnp.pad(adjoint, ((0, 0), (1, 1), (0, 0), (0, 0)))
    return grad_field(e_core, e_pad[:, :-2], e_pad[:, 2:], pressure, p_pad[:, :-2], p_pad[:, 2:], adjoint, q_pad[:, :-2], q_pad[:, 2:])

def reference(logperm, source, observed, brownian):
    blocks = logperm.reshape(J // PART_DEV, PART_DEV, NXG, NY, NZ)

    def per_block(block):
        return field_gradient(block, source[None], observed[None])
    gradient = lax.map(per_block, blocks).reshape(J, CELLS)
    members = logperm.reshape(J, CELLS)
    centre = lax.optimization_barrier(jnp.mean(members, axis=0, keepdims=True))
    spread = members - centre
    gram = jnp.dot(spread, gradient.T, precision=lax.Precision.HIGHEST, preferred_element_type=jnp.float32)
    step_size = J / (4.0 * (CELLS + 1))
    mixing = -(step_size / J) * gram + math.sqrt(2.0 * step_size / J) * brownian
    moved = centre + 1.25 * spread + jnp.dot(mixing.T, spread, precision=lax.Precision.HIGHEST, preferred_element_type=jnp.float32)
    return moved.reshape(logperm.shape)
```

```python
import math

import jax
import jax.numpy as jnp
from jax import lax
from jax.experimental import pallas as pl
from jax.experimental.pallas import tpu as pltpu
from jax.sharding import Mesh
from jax.sharding import PartitionSpec as P

SWEEPS = 8
MISFIT_WEIGHT = 1000.0
PAD = 8


def darcy_kernel(u_ref, src_ref, obs_ref, g_ref, e_s, w0, w1, inv_s, b_s, a_s, p_s):
    layers, rows, lanes = u_ref.shape
    lane = lax.broadcasted_iota(jnp.int32, (rows, lanes), 1)
    first = lane == 0
    last = lane == lanes - 1
    mid = pl.ds(PAD, rows)
    up = pl.ds(PAD - 1, rows)
    down = pl.ds(PAD + 1, rows)

    def before(v, fill):
        return jnp.where(first, fill, pltpu.roll(v, 1, 1))

    def after(v, fill):
        return jnp.where(last, fill, pltpu.roll(v, lanes - 1, 1))

    def each_layer(body):
        def step(i, carry):
            body(i)
            return carry

        lax.fori_loop(0, layers, step, 0, unroll=2)

    def neighbors(ref, i, fill):
        core = ref[i + 1, mid, :]
        return (
            (ref[i, mid, :] + ref[i + 2, mid, :])
            + (ref[i + 1, up, :] + ref[i + 1, down, :])
            + (before(core, fill) + after(core, fill))
        )

    e_s[...] = jnp.ones_like(e_s)
    w0[...] = jnp.zeros_like(w0)
    w1[...] = jnp.zeros_like(w1)
    p_s[...] = jnp.zeros_like(p_s)

    def fill_e(i):
        e_s[i + 1, mid, :] = jnp.exp(0.5 * u_ref[i])

    each_layer(fill_e)

    def fill_inv(i):
        inverse = 1.0 / neighbors(e_s, i, 1.0)
        inv_s[i] = inverse
        b_s[i] = inverse * e_s[i + 1, mid, :]
        start = inverse * src_ref[i]
        a_s[i] = start
        w0[i + 1, mid, :] = start

    each_layer(fill_inv)

    def relax():
        now, new = w0, w1
        for _ in range(SWEEPS - 1):

            def sweep(i, now=now, new=new):
                new[i + 1, mid, :] = a_s[i] + b_s[i] * neighbors(now, i, 0.0)

            each_layer(sweep)
            now, new = new, now
        return now

    end = relax()

    def to_adjoint(i):
        pressure = end[i + 1, mid, :] / e_s[i + 1, mid, :]
        p_s[i + 1, mid, :] = pressure
        start = inv_s[i] * (MISFIT_WEIGHT * (pressure - obs_ref[i]))
        a_s[i] = start
        w0[i + 1, mid, :] = start

    each_layer(to_adjoint)
    end = relax()

    def to_pressure(i):
        end[i + 1, mid, :] = end[i + 1, mid, :] / e_s[i + 1, mid, :]

    each_layer(to_pressure)

    def gradient(i):
        e = e_s[i + 1, mid, :]
        p = p_s[i + 1, mid, :]
        q = end[i + 1, mid, :]
        total = None
        for at, where in ((i, mid), (i + 2, mid), (i + 1, up), (i + 1, down)):
            term = e_s[at, where, :] * (p - p_s[at, where, :]) * (q - end[at, where, :])
            total = term if total is None else total + term
        for shift in (before, after):
            total = total + shift(e, 1.0) * (p - shift(p, 0.0)) * (q - shift(q, 0.0))
        return -0.5 * e * total

    slabs = layers // 4

    def write(s, carry):
        for b in range(4):
            g_ref[b * slabs + s] = gradient(s * 4 + b)
        return carry

    lax.fori_loop(0, slabs, write, 0)


def darcy(u, source, observed):
    layers, rows, lanes = u.shape
    padded = pltpu.VMEM((layers + 2, rows + 2 * PAD, lanes), jnp.float32)
    plain = pltpu.VMEM((layers, rows, lanes), jnp.float32)
    return pl.pallas_call(
        darcy_kernel,
        out_shape=jax.ShapeDtypeStruct(u.shape, jnp.float32),
        scratch_shapes=[padded, padded, padded, plain, plain, plain, padded],
        compiler_params=pltpu.CompilerParams(vmem_limit_bytes=24 << 20),
        name="darcy",
    )(u, source, observed)


def split(v):
    high = v.astype(jnp.bfloat16)
    low = (v - high.astype(jnp.float32)).astype(jnp.bfloat16)
    return high, low


def gram_kernel(u_ref, g_ref, o_ref):
    @pl.when(pl.program_id(0) == 0)
    def _():
        o_ref[...] = jnp.zeros_like(o_ref)

    members = u_ref.shape[0]
    block = g_ref.shape[0]
    u = u_ref[...]
    s = u - jnp.sum(u, axis=0, keepdims=True) * (1.0 / members)
    s_high, s_low = split(s)
    pair = jnp.concatenate(split(g_ref[...]), axis=0)
    dims = (((1,), (1,)), ((), ()))
    out = lax.dot_general(pair, s_high, dims, preferred_element_type=jnp.float32)
    out = out + lax.dot_general(pair, s_low, dims, preferred_element_type=jnp.float32)
    o_ref[...] += out[:block] + out[block:]


def gram_product(u_all, g, tile):
    members, cells = u_all.shape
    block = g.shape[0]
    return pl.pallas_call(
        gram_kernel,
        grid=(cells // tile,),
        in_specs=[
            pl.BlockSpec((members, tile), lambda i: (0, i)),
            pl.BlockSpec((block, tile), lambda i: (0, i)),
        ],
        out_specs=pl.BlockSpec((block, members), lambda i: (0, 0)),
        out_shape=jax.ShapeDtypeStruct((block, members), jnp.float32),
        compiler_params=pltpu.CompilerParams(vmem_limit_bytes=24 << 20),
        name="gram",
    )(u_all, g)


def move_kernel(u_ref, own_ref, m_ref, o_ref):
    members = u_ref.shape[0]
    block, groups, lanes = o_ref.shape
    u = u_ref[...]
    centre = jnp.sum(u, axis=0, keepdims=True) * (1.0 / members)
    s_high, s_low = split(u - centre)
    pair = jnp.concatenate(split(m_ref[...]), axis=0)
    dims = (((1,), (0,)), ((), ()))
    out = lax.dot_general(pair, s_high, dims, preferred_element_type=jnp.float32)
    out = out + lax.dot_general(pair, s_low, dims, preferred_element_type=jnp.float32)
    moved = centre + 1.25 * (own_ref[...] - centre) + (out[:block] + out[block:])
    for r in range(groups):
        o_ref[:, r, :] = moved[:, r * lanes : (r + 1) * lanes]


def move(u_all, own, mixing, tile):
    members, cells = u_all.shape
    block = own.shape[0]
    lanes = 128
    return pl.pallas_call(
        move_kernel,
        grid=(cells // tile,),
        in_specs=[
            pl.BlockSpec((members, tile), lambda i: (0, i)),
            pl.BlockSpec((block, tile), lambda i: (0, i)),
            pl.BlockSpec((block, members), lambda i: (0, 0)),
        ],
        out_specs=pl.BlockSpec((block, tile // lanes, lanes), lambda i: (0, i, 0)),
        out_shape=jax.ShapeDtypeStruct((block, cells // lanes, lanes), jnp.float32),
        compiler_params=pltpu.CompilerParams(vmem_limit_bytes=24 << 20),
        name="move",
    )(u_all, own, mixing)


def on_device(logperm, source, observed, brownian):
    particles, width, rows, lanes = logperm.shape
    slabs = lax.axis_size("y")
    xs = lax.axis_size("x")
    groups = lax.axis_size("z") * lax.axis_size("c")
    ensemble = particles * xs * groups
    layer = rows * lanes
    cells = width * slabs * layer

    chunks = jnp.swapaxes(logperm.reshape(particles, width, layer), 0, 1)
    own = lax.all_to_all(chunks, "x", split_axis=0, concat_axis=0, tiled=True)
    own = own.reshape(xs * particles, layer)
    u_all = lax.all_gather(own, ("z", "c"), axis=0, tiled=True)

    own_now, logperm_now = lax.optimization_barrier((own, logperm))
    shared = jnp.stack([source, observed])
    sent = jnp.concatenate(
        [logperm_now[:, None], jnp.broadcast_to(shared[None], (particles,) + shared.shape)], axis=1
    )
    whole = lax.all_to_all(sent, "y", split_axis=0, concat_axis=0, tiled=True)
    whole = jnp.swapaxes(whole, 0, 1).reshape(3, slabs * width, rows, lanes)
    gradient = darcy(whole[0], whole[1], whole[2])
    g = lax.all_to_all(gradient, ("x", "y"), split_axis=0, concat_axis=0, tiled=True)
    g = g.reshape(xs * particles, layer)

    step_size = ensemble / (4.0 * (cells + 1))
    noise = brownian.reshape(xs, groups, particles, xs, groups, particles)
    noise = lax.dynamic_index_in_dim(noise, lax.axis_index(("z", "c")), axis=4, keepdims=False)
    noise = jnp.transpose(noise, (3, 4, 1, 0, 2)).reshape(xs * particles, ensemble)
    noise = math.sqrt(2.0 * step_size / ensemble) * noise

    part = gram_product(u_all, g, 1024)
    copies = jnp.broadcast_to(part[None], (xs * slabs,) + part.shape)
    gram = jnp.sum(lax.all_to_all(copies, ("x", "y"), split_axis=0, concat_axis=0, tiled=True), axis=0)
    mixing = -(step_size / ensemble) * gram + noise
    moved = move(u_all, own_now, mixing, 1024)
    moved = moved.reshape(xs, particles, rows, lanes)
    returned = lax.all_to_all(moved, "x", split_axis=0, concat_axis=0, tiled=True)
    return jnp.swapaxes(returned, 0, 1)


def solution(mesh):
    fine = Mesh(mesh.devices.reshape(4, 8, 2, 4), ("x", "z", "c", "y"))
    dom = ("x", "z", "c")
    return jax.shard_map(
        on_device,
        mesh=fine,
        in_specs=(P(dom, "y", None, None), P("y", None, None), P("y", None, None), P()),
        out_specs=P(dom, "y", None, None),
        check_vma=False,
    )
```

```python
import math

import jax
import jax.numpy as jnp
from jax import lax
from jax.experimental import pallas as pl
from jax.experimental.pallas import tpu as pltpu
from jax.sharding import Mesh
from jax.sharding import PartitionSpec as P

SWEEPS = 8
MISFIT_WEIGHT = 1000.0
PAD = 8


def darcy_kernel(u_ref, src_ref, obs_ref, g_ref, e_s, w0, w1, inv_s, b_s, a_s, p_s):
    layers, rows, lanes = u_ref.shape
    lane = lax.broadcasted_iota(jnp.int32, (rows, lanes), 1)
    first = lane == 0
    last = lane == lanes - 1
    mid = pl.ds(PAD, rows)
    up = pl.ds(PAD - 1, rows)
    down = pl.ds(PAD + 1, rows)

    def before(v, fill):
        return jnp.where(first, fill, pltpu.roll(v, 1, 1))

    def after(v, fill):
        return jnp.where(last, fill, pltpu.roll(v, lanes - 1, 1))

    def each_layer(body):
        def step(i, carry):
            body(i)
            return carry

        lax.fori_loop(0, layers, step, 0, unroll=2)

    def neighbors(ref, i, fill):
        core = ref[i + 1, mid, :]
        return (
            (ref[i, mid, :] + ref[i + 2, mid, :])
            + (ref[i + 1, up, :] + ref[i + 1, down, :])
            + (before(core, fill) + after(core, fill))
        )

    e_s[...] = jnp.ones_like(e_s)
    w0[...] = jnp.zeros_like(w0)
    w1[...] = jnp.zeros_like(w1)
    p_s[...] = jnp.zeros_like(p_s)

    def fill_e(i):
        e_s[i + 1, mid, :] = jnp.exp(0.5 * u_ref[i])

    each_layer(fill_e)

    def fill_inv(i):
        inverse = 1.0 / neighbors(e_s, i, 1.0)
        inv_s[i] = inverse
        b_s[i] = inverse * e_s[i + 1, mid, :]
        start = inverse * src_ref[i]
        a_s[i] = start
        w0[i + 1, mid, :] = start

    each_layer(fill_inv)

    def relax():
        now, new = w0, w1
        for _ in range(SWEEPS - 1):

            def sweep(i, now=now, new=new):
                new[i + 1, mid, :] = a_s[i] + b_s[i] * neighbors(now, i, 0.0)

            each_layer(sweep)
            now, new = new, now
        return now

    end = relax()

    def to_adjoint(i):
        pressure = end[i + 1, mid, :] / e_s[i + 1, mid, :]
        p_s[i + 1, mid, :] = pressure
        start = inv_s[i] * (MISFIT_WEIGHT * (pressure - obs_ref[i]))
        a_s[i] = start
        w0[i + 1, mid, :] = start

    each_layer(to_adjoint)
    end = relax()

    def to_pressure(i):
        end[i + 1, mid, :] = end[i + 1, mid, :] / e_s[i + 1, mid, :]

    each_layer(to_pressure)

    def gradient(i):
        e = e_s[i + 1, mid, :]
        p = p_s[i + 1, mid, :]
        q = end[i + 1, mid, :]
        total = None
        for at, where in ((i, mid), (i + 2, mid), (i + 1, up), (i + 1, down)):
            term = e_s[at, where, :] * (p - p_s[at, where, :]) * (q - end[at, where, :])
            total = term if total is None else total + term
        for shift in (before, after):
            total = total + shift(e, 1.0) * (p - shift(p, 0.0)) * (q - shift(q, 0.0))
        return -0.5 * e * total

    slabs = layers // 4

    def write(s, carry):
        for b in range(4):
            g_ref[b * slabs + s] = gradient(s * 4 + b)
        return carry

    lax.fori_loop(0, slabs, write, 0)


def darcy(u, source, observed):
    layers, rows, lanes = u.shape
    padded = pltpu.VMEM((layers + 2, rows + 2 * PAD, lanes), jnp.float32)
    plain = pltpu.VMEM((layers, rows, lanes), jnp.float32)
    return pl.pallas_call(
        darcy_kernel,
        out_shape=jax.ShapeDtypeStruct(u.shape, jnp.float32),
        scratch_shapes=[padded, padded, padded, plain, plain, plain, padded],
        compiler_params=pltpu.CompilerParams(vmem_limit_bytes=24 << 20),
        name="darcy",
    )(u, source, observed)


def split(v):
    high = v.astype(jnp.bfloat16)
    low = (v - high.astype(jnp.float32)).astype(jnp.bfloat16)
    return high, low


def rows_of(ref, r):
    members, groups, lanes = ref.shape
    return ref.reshape(members * groups, lanes)[pl.ds(r, members, stride=groups), :]


def flat(ref):
    return jnp.concatenate([rows_of(ref, r) for r in range(ref.shape[1])], axis=1)


def gram_kernel(u_ref, g_ref, o_ref, acc):
    step = pl.program_id(0)

    @pl.when(step == 0)
    def _():
        acc[...] = jnp.zeros_like(acc)

    members = u_ref.shape[0]
    block = g_ref.shape[0]
    u = flat(u_ref)
    s = u - jnp.sum(u, axis=0, keepdims=True) * (1.0 / members)
    s_high, s_low = split(s)
    pair = jnp.concatenate(split(flat(g_ref)), axis=0)
    dims = (((1,), (1,)), ((), ()))
    out = lax.dot_general(pair, s_high, dims, preferred_element_type=jnp.float32)
    out = out + lax.dot_general(pair, s_low, dims, preferred_element_type=jnp.float32)
    acc[...] += out[:block] + out[block:]

    @pl.when(step == pl.num_programs(0) - 1)
    def _():
        for d in range(o_ref.shape[0]):
            o_ref[d] = acc[...]


def gram_product(u_all, g, copies, groups):
    members, rows, lanes = u_all.shape
    block = g.shape[0]
    return pl.pallas_call(
        gram_kernel,
        grid=(rows // groups,),
        in_specs=[
            pl.BlockSpec((members, groups, lanes), lambda i: (0, i, 0)),
            pl.BlockSpec((block, groups, lanes), lambda i: (0, i, 0)),
        ],
        out_specs=pl.BlockSpec((copies, block, members), lambda i: (0, 0, 0)),
        out_shape=jax.ShapeDtypeStruct((copies, block, members), jnp.float32),
        scratch_shapes=[pltpu.VMEM((block, members), jnp.float32)],
        compiler_params=pltpu.CompilerParams(vmem_limit_bytes=24 << 20),
        name="gram",
    )(u_all, g)


def move_kernel(u_ref, own_ref, parts_ref, noise_ref, o_ref, pair_s, *, scale):
    @pl.when(pl.program_id(0) == 0)
    def _():
        total = parts_ref[0]
        for d in range(1, parts_ref.shape[0]):
            total = total + parts_ref[d]
        pair_s[...] = jnp.concatenate(split(noise_ref[...] - scale * total), axis=0)

    members = u_ref.shape[0]
    block, groups, lanes = o_ref.shape
    u = flat(u_ref)
    centre = jnp.sum(u, axis=0, keepdims=True) * (1.0 / members)
    s_high, s_low = split(u - centre)
    dims = (((1,), (0,)), ((), ()))
    out = lax.dot_general(pair_s[...], s_high, dims, preferred_element_type=jnp.float32)
    out = out + lax.dot_general(pair_s[...], s_low, dims, preferred_element_type=jnp.float32)
    moved = centre + 1.25 * (flat(own_ref) - centre) + (out[:block] + out[block:])
    rows = o_ref.reshape(block * groups, lanes)
    for r in range(groups):
        rows[pl.ds(r, block, stride=groups), :] = moved[:, r * lanes : (r + 1) * lanes]


def move(u_all, own, parts, noise, scale, groups):
    members, rows, lanes = u_all.shape
    block = own.shape[0]
    return pl.pallas_call(
        lambda *refs: move_kernel(*refs, scale=scale),
        grid=(rows // groups,),
        in_specs=[
            pl.BlockSpec((members, groups, lanes), lambda i: (0, i, 0)),
            pl.BlockSpec((block, groups, lanes), lambda i: (0, i, 0)),
            pl.BlockSpec(parts.shape, lambda i: (0, 0, 0)),
            pl.BlockSpec(noise.shape, lambda i: (0, 0)),
        ],
        out_specs=pl.BlockSpec((block, groups, lanes), lambda i: (0, i, 0)),
        out_shape=jax.ShapeDtypeStruct((block, rows, lanes), jnp.float32),
        scratch_shapes=[pltpu.VMEM((2 * block, members), jnp.bfloat16)],
        compiler_params=pltpu.CompilerParams(vmem_limit_bytes=24 << 20),
        name="move",
    )(u_all, own, parts, noise)


def noise_kernel(at_ref, b_ref, o_ref, *, xs, groups, particles, scale):
    block, members = o_ref.shape
    per_x = groups * particles
    t = lax.broadcasted_iota(jnp.int32, (block, members), 0)
    j = lax.broadcasted_iota(jnp.int32, (block, members), 1)
    column = (t // particles) * per_x + at_ref[0] * particles + t % particles
    chosen = jnp.where(j == column, scale, 0.0)
    k = lax.broadcasted_iota(jnp.int32, (members, members), 0)
    m = lax.broadcasted_iota(jnp.int32, (members, members), 1)
    row = ((m // particles) % xs) * per_x + (m // (xs * particles)) * particles + m % particles
    order = jnp.where(k == row, 1.0, 0.0)
    picked = lax.dot_general(
        chosen, b_ref[...], (((1,), (1,)), ((), ())),
        precision=lax.Precision.HIGHEST, preferred_element_type=jnp.float32,
    )
    o_ref[...] = lax.dot_general(
        picked, order, (((1,), (0,)), ((), ())),
        precision=lax.Precision.HIGHEST, preferred_element_type=jnp.float32,
    )


def ordered_noise(brownian, at, xs, groups, particles, scale):
    return pl.pallas_call(
        lambda *refs: noise_kernel(*refs, xs=xs, groups=groups, particles=particles, scale=scale),
        in_specs=[
            pl.BlockSpec(memory_space=pltpu.SMEM),
            pl.BlockSpec(memory_space=pltpu.VMEM),
        ],
        out_shape=jax.ShapeDtypeStruct((xs * particles, brownian.shape[0]), jnp.float32),
        compiler_params=pltpu.CompilerParams(vmem_limit_bytes=24 << 20),
        name="noise",
    )(at.reshape(1), brownian)


def on_device(logperm, source, observed, brownian):
    particles, width, rows, lanes = logperm.shape
    slabs = lax.axis_size("y")
    xs = lax.axis_size("x")
    groups = lax.axis_size("z") * lax.axis_size("c")
    ensemble = particles * xs * groups
    layer = rows * lanes
    cells = width * slabs * layer

    chunks = jnp.swapaxes(logperm, 0, 1)
    own = lax.all_to_all(chunks, "x", split_axis=0, concat_axis=0, tiled=True)
    own = own.reshape(xs * particles, rows, lanes)
    u_all = lax.all_gather(own, ("z", "c"), axis=0, tiled=True)
    u_all = pltpu.with_memory_space_constraint(u_all, pltpu.HBM)

    own, logperm = lax.optimization_barrier((own, logperm))
    shared = jnp.stack([source, observed])
    sent = jnp.concatenate(
        [logperm[:, None], jnp.broadcast_to(shared[None], (particles,) + shared.shape)], axis=1
    )
    whole = lax.all_to_all(sent, "y", split_axis=0, concat_axis=0, tiled=True)
    whole = jnp.swapaxes(whole, 0, 1).reshape(3, slabs * width, rows, lanes)
    gradient = darcy(whole[0], whole[1], whole[2])
    g = lax.all_to_all(gradient, ("x", "y"), split_axis=0, concat_axis=0, tiled=True)

    step_size = ensemble / (4.0 * (cells + 1))
    at = lax.axis_index(("z", "c"))
    noise_scale = math.sqrt(2.0 * step_size / ensemble)
    noise = ordered_noise(brownian, at, xs, groups, particles, noise_scale)
    g, noise = lax.optimization_barrier((g, noise))

    parts = gram_product(u_all, g, xs * slabs, 8)
    parts = lax.all_to_all(parts, ("x", "y"), split_axis=0, concat_axis=0, tiled=True)
    moved = move(u_all, own, parts, noise, step_size / ensemble, 8)
    moved = moved.reshape(xs, particles, rows, lanes)
    returned = lax.all_to_all(moved, "x", split_axis=0, concat_axis=0, tiled=True)
    return jnp.swapaxes(returned, 0, 1)


def solution(mesh):
    fine = Mesh(mesh.devices.reshape(4, 8, 2, 4), ("x", "z", "c", "y"))
    dom = ("x", "z", "c")
    return jax.shard_map(
        on_device,
        mesh=fine,
        in_specs=(P(dom, "y", None, None), P("y", None, None), P("y", None, None), P()),
        out_specs=P(dom, "y", None, None),
        check_vma=False,
    )
```

```python
import math

import jax
import jax.numpy as jnp
from jax import lax
from jax.experimental import pallas as pl
from jax.experimental.pallas import tpu as pltpu
from jax.sharding import Mesh
from jax.sharding import PartitionSpec as P

SWEEPS = 8
MISFIT_WEIGHT = 1000.0
PAD = 8
SPREAD_AXIS = "x"
GATHER_AXES = ("z", "c")
VMEM_LIMIT = 32 << 20


def member(group, spot, particle):
    if SPREAD_AXIS == "x":
        return spot * 64 + group * 4 + particle
    return (group // 2) * 64 + spot * 8 + (group % 2) * 4 + particle


def darcy_kernel(
    y_ref, u_ref, src_ref, obs_ref, r1_ref, r2_ref, r3_ref, g_ref,
    e_s, w0, w1, p_s, inv_s, b_s, a_s, src_s, obs_s,
):
    slabs, width, rows, lanes = u_ref.shape
    layers = slabs * width
    lane = lax.broadcasted_iota(jnp.int32, (rows, lanes), 1)
    first = lane == 0
    last = lane == lanes - 1
    mid = pl.ds(PAD, rows)
    up = pl.ds(PAD - 1, rows)
    down = pl.ds(PAD + 1, rows)

    def before(v, fill):
        return jnp.where(first, fill, pltpu.roll(v, 1, 1))

    def after(v, fill):
        return jnp.where(last, fill, pltpu.roll(v, lanes - 1, 1))

    def neighbors(ref, i, fill):
        core = ref[i + 1, mid, :]
        return (
            (ref[i, mid, :] + ref[i + 2, mid, :])
            + (ref[i + 1, up, :] + ref[i + 1, down, :])
            + (before(core, fill) + after(core, fill))
        )

    for ref, fill in ((e_s, 1.0), (w0, 0.0), (w1, 0.0), (p_s, 0.0)):
        ref[:, :PAD, :] = jnp.full((layers + 2, PAD, lanes), fill, jnp.float32)
        ref[:, PAD + rows :, :] = jnp.full((layers + 2, PAD, lanes), fill, jnp.float32)
        for outside in (0, layers + 1):
            ref[outside, mid, :] = jnp.full((rows, lanes), fill, jnp.float32)

    y = y_ref[0]
    for w in range(width):
        e_s[y * width + w + 1, mid, :] = jnp.exp(0.5 * u_ref[y, w])
        src_s[y * width + w] = src_ref[w]
        obs_s[y * width + w] = obs_ref[w]
    for shift, ref in ((1, r1_ref), (2, r2_ref), (3, r3_ref)):
        slab = lax.rem(y + slabs - shift, slabs)
        for w in range(width):
            e_s[slab * width + w + 1, mid, :] = jnp.exp(0.5 * ref[0, w])
            src_s[slab * width + w] = ref[1, w]
            obs_s[slab * width + w] = ref[2, w]

    for i in range(layers):
        inverse = 1.0 / neighbors(e_s, i, 1.0)
        inv_s[i] = inverse
        b_s[i] = inverse * e_s[i + 1, mid, :]
        start = inverse * src_s[i]
        a_s[i] = start
        w0[i + 1, mid, :] = start

    def sweep(now, new):
        for i in range(layers):
            new[i + 1, mid, :] = a_s[i] + b_s[i] * neighbors(now, i, 0.0)

    def relax():
        def two(_, carry):
            sweep(w0, w1)
            sweep(w1, w0)
            return carry

        lax.fori_loop(0, (SWEEPS - 1) // 2, two, 0)
        sweep(w0, w1)

    relax()
    for i in range(layers):
        pressure = w1[i + 1, mid, :] / e_s[i + 1, mid, :]
        p_s[i + 1, mid, :] = pressure
        start = inv_s[i] * (MISFIT_WEIGHT * (pressure - obs_s[i]))
        a_s[i] = start
        w0[i + 1, mid, :] = start
    relax()
    for i in range(layers):
        w1[i + 1, mid, :] = w1[i + 1, mid, :] / e_s[i + 1, mid, :]

    chunk = g_ref.shape[1]
    per_layer = rows // chunk
    for i in range(layers):
        e = e_s[i + 1, mid, :]
        p = p_s[i + 1, mid, :]
        q = w1[i + 1, mid, :]
        total = None
        for at, where in ((i, mid), (i + 2, mid), (i + 1, up), (i + 1, down)):
            term = e_s[at, where, :] * (p - p_s[at, where, :]) * (q - w1[at, where, :])
            total = term if total is None else total + term
        for shift in (before, after):
            total = total + shift(e, 1.0) * (p - shift(p, 0.0)) * (q - shift(q, 0.0))
        gradient = -0.5 * e * total
        for h in range(per_layer):
            spot = (i % width) * per_layer + h
            g_ref[spot * slabs + i // width] = gradient[h * chunk : (h + 1) * chunk]


def darcy(y, u, source, observed, received, chunk):
    slabs, width, rows, lanes = u.shape
    layers = slabs * width
    padded = pltpu.VMEM((layers + 2, rows + 2 * PAD, lanes), jnp.float32)
    plain = pltpu.VMEM((layers, rows, lanes), jnp.float32)
    whole = pl.BlockSpec(memory_space=pltpu.VMEM)
    return pl.pallas_call(
        darcy_kernel,
        in_specs=[pl.BlockSpec(memory_space=pltpu.SMEM)] + [whole] * 6,
        out_specs=whole,
        out_shape=jax.ShapeDtypeStruct((layers * rows // chunk, chunk, lanes), jnp.float32),
        scratch_shapes=[padded] * 4 + [plain] * 5,
        compiler_params=pltpu.CompilerParams(vmem_limit_bytes=VMEM_LIMIT),
        name="darcy",
    )(y.reshape(1), u, source, observed, *received)


def split(v):
    high = v.astype(jnp.bfloat16)
    low = (v - high.astype(jnp.float32)).astype(jnp.bfloat16)
    return high, low


def gram_kernel(u_ref, g_ref, o_ref):
    @pl.when(pl.program_id(0) == 0)
    def _():
        o_ref[...] = jnp.zeros_like(o_ref)

    members = u_ref.shape[0]
    block = g_ref.shape[0]
    u = u_ref[...]
    s = u - jnp.sum(u, axis=0, keepdims=True) * (1.0 / members)
    s_high, s_low = split(s)
    pair = jnp.concatenate(split(g_ref[...]), axis=0)
    dims = (((1,), (1,)), ((), ()))
    out = lax.dot_general(pair, s_high, dims, preferred_element_type=jnp.float32)
    out = out + lax.dot_general(pair, s_low, dims, preferred_element_type=jnp.float32)
    o_ref[...] += out[:block] + out[block:]


def gram_product(u_all, g, tile):
    members, cells = u_all.shape
    block = g.shape[0]
    return pl.pallas_call(
        gram_kernel,
        grid=(cells // tile,),
        in_specs=[
            pl.BlockSpec((members, tile), lambda i: (0, i)),
            pl.BlockSpec((block, tile), lambda i: (0, i)),
        ],
        out_specs=pl.BlockSpec((block, members), lambda i: (0, 0)),
        out_shape=jax.ShapeDtypeStruct((block, members), jnp.float32),
        compiler_params=pltpu.CompilerParams(vmem_limit_bytes=VMEM_LIMIT),
        name="gram",
    )(u_all, g)


def move_kernel(u_ref, own_ref, parts_ref, noise_ref, o_ref, pair_s, *, scale):
    @pl.when(pl.program_id(0) == 0)
    def _():
        total = parts_ref[0]
        for d in range(1, parts_ref.shape[0]):
            total = total + parts_ref[d]
        pair_s[...] = jnp.concatenate(split(noise_ref[...] - scale * total), axis=0)

    members = u_ref.shape[0]
    block, groups, lanes = o_ref.shape
    u = u_ref[...]
    centre = jnp.sum(u, axis=0, keepdims=True) * (1.0 / members)
    s_high, s_low = split(u - centre)
    dims = (((1,), (0,)), ((), ()))
    out = lax.dot_general(pair_s[...], s_high, dims, preferred_element_type=jnp.float32)
    out = out + lax.dot_general(pair_s[...], s_low, dims, preferred_element_type=jnp.float32)
    moved = centre + 1.25 * (own_ref[...] - centre) + (out[:block] + out[block:])
    for r in range(groups):
        o_ref[:, r, :] = moved[:, r * lanes : (r + 1) * lanes]


def move(u_all, own, parts, noise, scale, tile):
    members, cells = u_all.shape
    block = own.shape[0]
    lanes = 128
    return pl.pallas_call(
        lambda *refs: move_kernel(*refs, scale=scale),
        grid=(cells // tile,),
        in_specs=[
            pl.BlockSpec((members, tile), lambda i: (0, i)),
            pl.BlockSpec((block, tile), lambda i: (0, i)),
            pl.BlockSpec(parts.shape, lambda i: (0, 0, 0)),
            pl.BlockSpec(noise.shape, lambda i: (0, 0)),
        ],
        out_specs=pl.BlockSpec((block, tile // lanes, lanes), lambda i: (0, i, 0)),
        out_shape=jax.ShapeDtypeStruct((block, cells // lanes, lanes), jnp.float32),
        scratch_shapes=[pltpu.VMEM((2 * block, members), jnp.bfloat16)],
        compiler_params=pltpu.CompilerParams(vmem_limit_bytes=VMEM_LIMIT),
        name="move",
    )(u_all, own, parts, noise)


def noise_kernel(at_ref, b_ref, o_ref, *, spots, particles, scale):
    block, members = o_ref.shape
    t = lax.broadcasted_iota(jnp.int32, (block, members), 0)
    j = lax.broadcasted_iota(jnp.int32, (block, members), 1)
    column = member(at_ref[0], t // particles, t % particles)
    chosen = jnp.where(j == column, scale, 0.0)
    k = lax.broadcasted_iota(jnp.int32, (members, members), 0)
    m = lax.broadcasted_iota(jnp.int32, (members, members), 1)
    row = member(m // (spots * particles), (m // particles) % spots, m % particles)
    order = jnp.where(k == row, 1.0, 0.0)
    picked = lax.dot_general(
        chosen, b_ref[...], (((1,), (1,)), ((), ())),
        precision=lax.Precision.HIGHEST, preferred_element_type=jnp.float32,
    )
    o_ref[...] = lax.dot_general(
        picked, order, (((1,), (0,)), ((), ())),
        precision=lax.Precision.HIGHEST, preferred_element_type=jnp.float32,
    )


def ordered_noise(brownian, at, spots, particles, scale):
    return pl.pallas_call(
        lambda *refs: noise_kernel(*refs, spots=spots, particles=particles, scale=scale),
        in_specs=[
            pl.BlockSpec(memory_space=pltpu.SMEM),
            pl.BlockSpec(memory_space=pltpu.VMEM),
        ],
        out_shape=jax.ShapeDtypeStruct((spots * particles, brownian.shape[0]), jnp.float32),
        compiler_params=pltpu.CompilerParams(vmem_limit_bytes=VMEM_LIMIT),
        name="noise",
    )(at.reshape(1), brownian)


def shifted(block, axis, shift):
    count = lax.axis_size(axis)
    return lax.ppermute(block, axis, [(i, (i + shift) % count) for i in range(count)])


def on_device(logperm, source, observed, brownian):
    particles, width, rows, lanes = logperm.shape
    slabs = lax.axis_size("y")
    spots = lax.axis_size(SPREAD_AXIS)
    ensemble = particles * spots * lax.axis_size(GATHER_AXES)
    chunk = width * rows // spots
    cells = width * slabs * rows * lanes

    y = lax.axis_index("y")
    fields = jnp.stack([source, observed])
    received = []
    for shift in range(1, slabs):
        mine = lax.dynamic_slice_in_dim(logperm, (y + shift) % slabs, 1, axis=0)
        received.append(shifted(jnp.concatenate([mine, fields], axis=0), "y", shift))

    chunks = jnp.swapaxes(logperm.reshape(particles, spots, chunk, lanes), 0, 1)
    own = lax.all_to_all(chunks, SPREAD_AXIS, split_axis=0, concat_axis=0, tiled=True)
    own = own.reshape(spots * particles, chunk * lanes)
    u_all = lax.all_gather(own, GATHER_AXES, axis=0, tiled=True)
    u_all = pltpu.with_memory_space_constraint(u_all, pltpu.HBM)

    gradient = darcy(y, logperm, source, observed, received, chunk)
    g = lax.all_to_all(gradient, (SPREAD_AXIS, "y"), split_axis=0, concat_axis=0, tiled=True)
    g = g.reshape(spots * particles, chunk * lanes)

    step_size = ensemble / (4.0 * (cells + 1))
    noise_scale = math.sqrt(2.0 * step_size / ensemble)
    noise = ordered_noise(brownian, lax.axis_index(GATHER_AXES), spots, particles, noise_scale)
    g, noise = lax.optimization_barrier((g, noise))

    tile = chunk * lanes // 2
    part = gram_product(u_all, g, tile)
    parts = jnp.broadcast_to(part[None], (spots * slabs,) + part.shape)
    parts = lax.all_to_all(parts, (SPREAD_AXIS, "y"), split_axis=0, concat_axis=0, tiled=True)
    moved = move(u_all, own, parts, noise, step_size / ensemble, tile)
    moved = moved.reshape(spots, particles, chunk, lanes)
    returned = lax.all_to_all(moved, SPREAD_AXIS, split_axis=0, concat_axis=0, tiled=True)
    return jnp.swapaxes(returned, 0, 1).reshape(logperm.shape)


def solution(mesh):
    fine = Mesh(mesh.devices.reshape(4, 8, 2, 4), ("x", "z", "c", "y"))
    dom = ("x", "z", "c")
    return jax.shard_map(
        on_device,
        mesh=fine,
        in_specs=(P(dom, "y", None, None), P("y", None, None), P("y", None, None), P()),
        out_specs=P(dom, "y", None, None),
        check_vma=False,
    )
```

```python
import math

import jax
import jax.numpy as jnp
from jax import lax
from jax.experimental import pallas as pl
from jax.experimental.pallas import tpu as pltpu
from jax.sharding import Mesh
from jax.sharding import PartitionSpec as P

SWEEPS = 8
MISFIT_WEIGHT = 1000.0
PAD = 8
SPREAD_AXES = ("x", "zh")
VMEM_LIMIT = 40 << 20


def offset(order):
    half = (order + 1) // 2
    return jnp.where(order % 2 == 0, half, -half)


def member(zl, core, spot, particle):
    return (spot // 2) * 64 + (zl * 2 + spot % 2) * 8 + core * 4 + particle


def darcy_kernel(
    y_ref, u_ref, src_ref, obs_ref, r1_ref, r2_ref, r3_ref, g_ref,
    e_s, w0, w1, p_s, inv_s, b_s, a_s, src_s, obs_s,
):
    slabs, width, rows, lanes = u_ref.shape
    layers = slabs * width
    lane = lax.broadcasted_iota(jnp.int32, (rows, lanes), 1)
    first = lane == 0
    last = lane == lanes - 1
    mid = pl.ds(PAD, rows)
    up = pl.ds(PAD - 1, rows)
    down = pl.ds(PAD + 1, rows)

    def before(v, fill):
        return jnp.where(first, fill, pltpu.roll(v, 1, 1))

    def after(v, fill):
        return jnp.where(last, fill, pltpu.roll(v, lanes - 1, 1))

    def neighbors(ref, i, fill):
        core = ref[i + 1, mid, :]
        return (
            (ref[i, mid, :] + ref[i + 2, mid, :])
            + (ref[i + 1, up, :] + ref[i + 1, down, :])
            + (before(core, fill) + after(core, fill))
        )

    for ref, fill in ((e_s, 1.0), (w0, 0.0), (w1, 0.0), (p_s, 0.0)):
        ref[:, :PAD, :] = jnp.full((layers + 2, PAD, lanes), fill, jnp.float32)
        ref[:, PAD + rows :, :] = jnp.full((layers + 2, PAD, lanes), fill, jnp.float32)
        for outside in (0, layers + 1):
            ref[outside, mid, :] = jnp.full((rows, lanes), fill, jnp.float32)

    y = y_ref[0]
    for w in range(width):
        e_s[y * width + w + 1, mid, :] = jnp.exp(0.5 * u_ref[y, w])
        src_s[y * width + w] = src_ref[w]
        obs_s[y * width + w] = obs_ref[w]
    for shift, ref in ((1, r1_ref), (2, r2_ref), (3, r3_ref)):
        slab = lax.rem(y + slabs - shift, slabs)
        for w in range(width):
            e_s[slab * width + w + 1, mid, :] = jnp.exp(0.5 * ref[0, w])
            src_s[slab * width + w] = ref[1, w]
            obs_s[slab * width + w] = ref[2, w]

    for i in range(layers):
        inverse = 1.0 / neighbors(e_s, i, 1.0)
        inv_s[i] = inverse
        b_s[i] = inverse * e_s[i + 1, mid, :]
        start = inverse * src_s[i]
        a_s[i] = start
        w0[i + 1, mid, :] = start

    def sweep(now, new):
        for i in range(layers):
            new[i + 1, mid, :] = a_s[i] + b_s[i] * neighbors(now, i, 0.0)

    def relax():
        def two(_, carry):
            sweep(w0, w1)
            sweep(w1, w0)
            return carry

        lax.fori_loop(0, (SWEEPS - 1) // 2, two, 0)
        sweep(w0, w1)

    relax()
    for i in range(layers):
        pressure = w1[i + 1, mid, :] / e_s[i + 1, mid, :]
        p_s[i + 1, mid, :] = pressure
        start = inv_s[i] * (MISFIT_WEIGHT * (pressure - obs_s[i]))
        a_s[i] = start
        w0[i + 1, mid, :] = start
    relax()
    for i in range(layers):
        w1[i + 1, mid, :] = w1[i + 1, mid, :] / e_s[i + 1, mid, :]

    chunk = g_ref.shape[1]
    per_layer = rows // chunk
    for i in range(layers):
        e = e_s[i + 1, mid, :]
        p = p_s[i + 1, mid, :]
        q = w1[i + 1, mid, :]
        total = None
        for at, where in ((i, mid), (i + 2, mid), (i + 1, up), (i + 1, down)):
            term = e_s[at, where, :] * (p - p_s[at, where, :]) * (q - w1[at, where, :])
            total = term if total is None else total + term
        for shift in (before, after):
            total = total + shift(e, 1.0) * (p - shift(p, 0.0)) * (q - shift(q, 0.0))
        gradient = -0.5 * e * total
        for h in range(per_layer):
            spot = (i % width) * per_layer + h
            g_ref[spot * slabs + i // width] = gradient[h * chunk : (h + 1) * chunk]


def darcy(y, u, source, observed, received, chunk):
    slabs, width, rows, lanes = u.shape
    layers = slabs * width
    padded = pltpu.VMEM((layers + 2, rows + 2 * PAD, lanes), jnp.float32)
    plain = pltpu.VMEM((layers, rows, lanes), jnp.float32)
    whole = pl.BlockSpec(memory_space=pltpu.VMEM)
    return pl.pallas_call(
        darcy_kernel,
        in_specs=[pl.BlockSpec(memory_space=pltpu.SMEM)] + [whole] * 6,
        out_specs=whole,
        out_shape=jax.ShapeDtypeStruct((layers * rows // chunk, chunk, lanes), jnp.float32),
        scratch_shapes=[padded] * 4 + [plain] * 5,
        compiler_params=pltpu.CompilerParams(vmem_limit_bytes=VMEM_LIMIT),
        name="darcy",
    )(y.reshape(1), u, source, observed, *received)


def split(v):
    high = v.astype(jnp.bfloat16)
    low = (v - high.astype(jnp.float32)).astype(jnp.bfloat16)
    return high, low


def columns(refs, start, size):
    return jnp.concatenate([ref[:, start : start + size] for ref in refs], axis=0)


def gram_kernel(*refs, tile):
    *u_refs, g_ref, o_ref = refs
    block, cells = g_ref.shape
    members = o_ref.shape[1]
    dims = (((1,), (1,)), ((), ()))
    total = jnp.zeros((2 * block, members), jnp.float32)
    for start in range(0, cells, tile):
        u = columns(u_refs, start, tile)
        s_high, s_low = split(u - jnp.sum(u, axis=0, keepdims=True) * (1.0 / members))
        pair = jnp.concatenate(split(g_ref[:, start : start + tile]), axis=0)
        total = total + lax.dot_general(pair, s_high, dims, preferred_element_type=jnp.float32)
        total = total + lax.dot_general(pair, s_low, dims, preferred_element_type=jnp.float32)
    o_ref[...] = total[:block] + total[block:]


def gram_product(blocks, g, tile):
    members = sum(b.shape[0] for b in blocks)
    whole = pl.BlockSpec(memory_space=pltpu.VMEM)
    return pl.pallas_call(
        lambda *refs: gram_kernel(*refs, tile=tile),
        in_specs=[whole] * (len(blocks) + 1),
        out_specs=whole,
        out_shape=jax.ShapeDtypeStruct((g.shape[0], members), jnp.float32),
        compiler_params=pltpu.CompilerParams(vmem_limit_bytes=VMEM_LIMIT),
        name="gram",
    )(*blocks, g)


def move_kernel(*refs, scale, tile):
    *u_refs, parts_ref, noise_ref, o_ref = refs
    block, _, lanes = o_ref.shape
    cells = u_refs[0].shape[1]
    members = noise_ref.shape[1]
    total = parts_ref[0]
    for d in range(1, parts_ref.shape[0]):
        total = total + parts_ref[d]
    pair = jnp.concatenate(split(noise_ref[...] - scale * total), axis=0)
    dims = (((1,), (0,)), ((), ()))
    for start in range(0, cells, tile):
        u = columns(u_refs, start, tile)
        s = u - jnp.sum(u, axis=0, keepdims=True) * (1.0 / members)
        s_high, s_low = split(s)
        out = lax.dot_general(pair, s_high, dims, preferred_element_type=jnp.float32)
        out = out + lax.dot_general(pair, s_low, dims, preferred_element_type=jnp.float32)
        moved = u[:block] + 0.25 * s[:block] + (out[:block] + out[block:])
        for r in range(tile // lanes):
            o_ref[:, start // lanes + r, :] = moved[:, r * lanes : (r + 1) * lanes]


def move(blocks, parts, noise, scale, tile):
    block, cells = blocks[0].shape
    lanes = 128
    whole = pl.BlockSpec(memory_space=pltpu.VMEM)
    return pl.pallas_call(
        lambda *refs: move_kernel(*refs, scale=scale, tile=tile),
        in_specs=[whole] * (len(blocks) + 2),
        out_specs=whole,
        out_shape=jax.ShapeDtypeStruct((block, cells // lanes, lanes), jnp.float32),
        compiler_params=pltpu.CompilerParams(vmem_limit_bytes=VMEM_LIMIT),
        name="move",
    )(*blocks, parts, noise)


def noise_kernel(at_ref, b_ref, o_ref, *, spots, particles, depth, scale):
    block, members = o_ref.shape
    zl, core = at_ref[0], at_ref[1]
    t = lax.broadcasted_iota(jnp.int32, (block, members), 0)
    j = lax.broadcasted_iota(jnp.int32, (block, members), 1)
    column = member(zl, core, t // particles, t % particles)
    chosen = jnp.where(j == column, scale, 0.0)
    k = lax.broadcasted_iota(jnp.int32, (members, members), 0)
    m = lax.broadcasted_iota(jnp.int32, (members, members), 1)
    order = (m // block) % depth
    m_zl = (zl + offset(order) + depth) % depth
    m_core = (core + m // (block * depth)) % 2
    row = member(m_zl, m_core, (m // particles) % spots, m % particles)
    chosen_row = jnp.where(k == row, 1.0, 0.0)
    picked = lax.dot_general(
        chosen, b_ref[...], (((1,), (1,)), ((), ())),
        precision=lax.Precision.HIGHEST, preferred_element_type=jnp.float32,
    )
    o_ref[...] = lax.dot_general(
        picked, chosen_row, (((1,), (0,)), ((), ())),
        precision=lax.Precision.HIGHEST, preferred_element_type=jnp.float32,
    )


def ordered_noise(brownian, at, spots, particles, depth, scale):
    return pl.pallas_call(
        lambda *refs: noise_kernel(
            *refs, spots=spots, particles=particles, depth=depth, scale=scale
        ),
        in_specs=[
            pl.BlockSpec(memory_space=pltpu.SMEM),
            pl.BlockSpec(memory_space=pltpu.VMEM),
        ],
        out_shape=jax.ShapeDtypeStruct((spots * particles, brownian.shape[0]), jnp.float32),
        compiler_params=pltpu.CompilerParams(vmem_limit_bytes=VMEM_LIMIT),
        name="noise",
    )(at, brownian)


def shifted(block, axis, shift):
    count = lax.axis_size(axis)
    return lax.ppermute(block, axis, [(i, (i + shift) % count) for i in range(count)])


def on_device(logperm, source, observed, brownian):
    particles, width, rows, lanes = logperm.shape
    slabs = lax.axis_size("y")
    spots = lax.axis_size(SPREAD_AXES)
    depth = lax.axis_size("zl")
    cores = lax.axis_size("c")
    ensemble = particles * spots * depth * cores
    chunk = width * rows // spots
    cells = width * slabs * rows * lanes

    chunks = jnp.swapaxes(logperm.reshape(particles, spots, chunk, lanes), 0, 1)
    own = lax.all_to_all(chunks, SPREAD_AXES, split_axis=0, concat_axis=0, tiled=True)
    own = own.reshape(spots * particles, chunk * lanes)

    y = lax.axis_index("y")
    fields = jnp.stack([source, observed])
    received = []
    for shift in range(1, slabs):
        mine = lax.dynamic_slice_in_dim(logperm, (y + shift) % slabs, 1, axis=0)
        received.append(shifted(jnp.concatenate([mine, fields], axis=0), "y", shift))

    blocks = [own]
    ahead, back = own, own
    for _ in range(depth // 2 - 1):
        ahead, back = shifted(ahead, "zl", 1), shifted(back, "zl", depth - 1)
        blocks += [ahead, back]
    half = own.shape[0] // 2
    blocks += [shifted(ahead[:half], "zl", 1), shifted(back[half:], "zl", depth - 1)]
    blocks += [shifted(block, "c", 1) for block in blocks]

    gradient = darcy(y, logperm, source, observed, received, chunk)
    g = lax.all_to_all(gradient, SPREAD_AXES + ("y",), split_axis=0, concat_axis=0, tiled=True)
    g = g.reshape(spots * particles, chunk * lanes)

    step_size = ensemble / (4.0 * (cells + 1))
    noise_scale = math.sqrt(2.0 * step_size / ensemble)
    at = jnp.stack([lax.axis_index("zl"), lax.axis_index("c")])
    noise = ordered_noise(brownian, at, spots, particles, depth, noise_scale)
    g, noise = lax.optimization_barrier((g, noise))

    part = gram_product(blocks, g, 1024)
    part = part + shifted(part, "zh", 1)
    copies = spots * slabs // 2
    parts = jnp.broadcast_to(part[None], (copies,) + part.shape)
    parts = lax.all_to_all(parts, ("x", "y"), split_axis=0, concat_axis=0, tiled=True)
    moved = move(blocks, parts, noise, step_size / ensemble, 1024)
    moved = moved.reshape(spots, particles, chunk, lanes)
    returned = lax.all_to_all(moved, SPREAD_AXES, split_axis=0, concat_axis=0, tiled=True)
    return jnp.swapaxes(returned, 0, 1).reshape(logperm.shape)


def solution(mesh):
    fine = Mesh(mesh.devices.reshape(4, 4, 2, 2, 4), ("x", "zl", "zh", "c", "y"))
    dom = ("x", "zl", "zh", "c")
    return jax.shard_map(
        on_device,
        mesh=fine,
        in_specs=(P(dom, "y", None, None), P("y", None, None), P("y", None, None), P()),
        out_specs=P(dom, "y", None, None),
        check_vma=False,
    )
```

```python
import math

import jax
import jax.numpy as jnp
from jax import lax
from jax.experimental import pallas as pl
from jax.experimental.pallas import tpu as pltpu
from jax.sharding import Mesh
from jax.sharding import PartitionSpec as P

SWEEPS = 8
MISFIT_WEIGHT = 1000.0
PAD = 8
SPREAD_AXES = ("x", "zh")
VMEM_LIMIT = 40 << 20


def offset(order):
    half = (order + 1) // 2
    return jnp.where(order % 2 == 0, half, -half)


def member(zl, core, spot, particle):
    return (spot // 2) * 64 + (zl * 2 + spot % 2) * 8 + core * 4 + particle


def darcy_kernel(
    y_ref, u_ref, src_ref, obs_ref, r1_ref, r2_ref, r3_ref, g_ref,
    e_s, w0, w1, p_s, inv_s, b_s, a_s, src_s, obs_s,
):
    slabs, width, rows, lanes = u_ref.shape
    layers = slabs * width
    lane = lax.broadcasted_iota(jnp.int32, (rows, lanes), 1)
    first = lane == 0
    last = lane == lanes - 1
    mid = pl.ds(PAD, rows)
    up = pl.ds(PAD - 1, rows)
    down = pl.ds(PAD + 1, rows)

    def before(v, fill):
        return jnp.where(first, fill, pltpu.roll(v, 1, 1))

    def after(v, fill):
        return jnp.where(last, fill, pltpu.roll(v, lanes - 1, 1))

    def neighbors(ref, i, fill):
        core = ref[i + 1, mid, :]
        return (
            (ref[i, mid, :] + ref[i + 2, mid, :])
            + (ref[i + 1, up, :] + ref[i + 1, down, :])
            + (before(core, fill) + after(core, fill))
        )

    for ref, fill in ((e_s, 1.0), (w0, 0.0), (w1, 0.0), (p_s, 0.0)):
        ref[:, :PAD, :] = jnp.full((layers + 2, PAD, lanes), fill, jnp.float32)
        ref[:, PAD + rows :, :] = jnp.full((layers + 2, PAD, lanes), fill, jnp.float32)
        for outside in (0, layers + 1):
            ref[outside, mid, :] = jnp.full((rows, lanes), fill, jnp.float32)

    y = y_ref[0]
    for w in range(width):
        e_s[y * width + w + 1, mid, :] = jnp.exp(0.5 * u_ref[y, w])
        src_s[y * width + w] = src_ref[w]
        obs_s[y * width + w] = obs_ref[w]
    for shift, ref in ((1, r1_ref), (2, r2_ref), (3, r3_ref)):
        slab = lax.rem(y + slabs - shift, slabs)
        for w in range(width):
            e_s[slab * width + w + 1, mid, :] = jnp.exp(0.5 * ref[0, w])
            src_s[slab * width + w] = ref[1, w]
            obs_s[slab * width + w] = ref[2, w]

    for i in range(layers):
        inverse = 1.0 / neighbors(e_s, i, 1.0)
        inv_s[i] = inverse
        b_s[i] = inverse * e_s[i + 1, mid, :]
        start = inverse * src_s[i]
        a_s[i] = start
        w0[i + 1, mid, :] = start

    def sweep(now, new):
        for i in range(layers):
            new[i + 1, mid, :] = a_s[i] + b_s[i] * neighbors(now, i, 0.0)

    def relax():
        def two(_, carry):
            sweep(w0, w1)
            sweep(w1, w0)
            return carry

        lax.fori_loop(0, (SWEEPS - 1) // 2, two, 0)
        sweep(w0, w1)

    relax()
    for i in range(layers):
        pressure = w1[i + 1, mid, :] / e_s[i + 1, mid, :]
        p_s[i + 1, mid, :] = pressure
        start = inv_s[i] * (MISFIT_WEIGHT * (pressure - obs_s[i]))
        a_s[i] = start
        w0[i + 1, mid, :] = start
    relax()
    for i in range(layers):
        w1[i + 1, mid, :] = w1[i + 1, mid, :] / e_s[i + 1, mid, :]

    chunk = g_ref.shape[1]
    per_layer = rows // chunk
    for i in range(layers):
        e = e_s[i + 1, mid, :]
        p = p_s[i + 1, mid, :]
        q = w1[i + 1, mid, :]
        total = None
        for at, where in ((i, mid), (i + 2, mid), (i + 1, up), (i + 1, down)):
            term = e_s[at, where, :] * (p - p_s[at, where, :]) * (q - w1[at, where, :])
            total = term if total is None else total + term
        for shift in (before, after):
            total = total + shift(e, 1.0) * (p - shift(p, 0.0)) * (q - shift(q, 0.0))
        gradient = -0.5 * e * total
        for h in range(per_layer):
            spot = (i % width) * per_layer + h
            g_ref[spot * slabs + i // width] = gradient[h * chunk : (h + 1) * chunk]


def darcy(y, u, source, observed, received, chunk):
    slabs, width, rows, lanes = u.shape
    layers = slabs * width
    padded = pltpu.VMEM((layers + 2, rows + 2 * PAD, lanes), jnp.float32)
    plain = pltpu.VMEM((layers, rows, lanes), jnp.float32)
    whole = pl.BlockSpec(memory_space=pltpu.VMEM)
    return pl.pallas_call(
        darcy_kernel,
        in_specs=[pl.BlockSpec(memory_space=pltpu.SMEM)] + [whole] * 6,
        out_specs=whole,
        out_shape=jax.ShapeDtypeStruct((layers * rows // chunk, chunk, lanes), jnp.float32),
        scratch_shapes=[padded] * 4 + [plain] * 5,
        compiler_params=pltpu.CompilerParams(vmem_limit_bytes=VMEM_LIMIT),
        name="darcy",
    )(y.reshape(1), u, source, observed, *received)


def split(v):
    high = v.astype(jnp.bfloat16)
    low = (v - high.astype(jnp.float32)).astype(jnp.bfloat16)
    return high, low


def columns(refs, start, size):
    return jnp.concatenate([ref[:, start : start + size] for ref in refs], axis=0)


def gram_kernel(*refs, tile):
    *u_refs, g_ref, o_ref = refs
    block, cells = g_ref.shape
    members = o_ref.shape[1]
    dims = (((1,), (1,)), ((), ()))
    total = jnp.zeros((2 * block, members), jnp.float32)
    for start in range(0, cells, tile):
        u = columns(u_refs, start, tile)
        s_high, s_low = split(u - jnp.sum(u, axis=0, keepdims=True) * (1.0 / members))
        pair = jnp.concatenate(split(g_ref[:, start : start + tile]), axis=0)
        total = total + lax.dot_general(pair, s_high, dims, preferred_element_type=jnp.float32)
        total = total + lax.dot_general(pair, s_low, dims, preferred_element_type=jnp.float32)
    o_ref[...] = total[:block] + total[block:]


def gram_product(blocks, g, tile):
    members = sum(b.shape[0] for b in blocks)
    whole = pl.BlockSpec(memory_space=pltpu.VMEM)
    return pl.pallas_call(
        lambda *refs: gram_kernel(*refs, tile=tile),
        in_specs=[whole] * (len(blocks) + 1),
        out_specs=whole,
        out_shape=jax.ShapeDtypeStruct((g.shape[0], members), jnp.float32),
        compiler_params=pltpu.CompilerParams(vmem_limit_bytes=VMEM_LIMIT),
        name="gram",
    )(*blocks, g)


def move_kernel(*refs, scale, tile):
    *u_refs, parts_ref, noise_ref, o_ref = refs
    block, _, lanes = o_ref.shape
    cells = u_refs[0].shape[1]
    members = noise_ref.shape[1]
    total = parts_ref[0]
    for d in range(1, parts_ref.shape[0]):
        total = total + parts_ref[d]
    pair = jnp.concatenate(split(noise_ref[...] - scale * total), axis=0)
    dims = (((1,), (0,)), ((), ()))
    for start in range(0, cells, tile):
        u = columns(u_refs, start, tile)
        s = u - jnp.sum(u, axis=0, keepdims=True) * (1.0 / members)
        s_high, s_low = split(s)
        out = lax.dot_general(pair, s_high, dims, preferred_element_type=jnp.float32)
        out = out + lax.dot_general(pair, s_low, dims, preferred_element_type=jnp.float32)
        moved = u[:block] + 0.25 * s[:block] + (out[:block] + out[block:])
        for r in range(tile // lanes):
            o_ref[:, start // lanes + r, :] = moved[:, r * lanes : (r + 1) * lanes]


def move(blocks, parts, noise, scale, tile):
    block, cells = blocks[0].shape
    lanes = 128
    whole = pl.BlockSpec(memory_space=pltpu.VMEM)
    return pl.pallas_call(
        lambda *refs: move_kernel(*refs, scale=scale, tile=tile),
        in_specs=[whole] * (len(blocks) + 2),
        out_specs=whole,
        out_shape=jax.ShapeDtypeStruct((block, cells // lanes, lanes), jnp.float32),
        compiler_params=pltpu.CompilerParams(vmem_limit_bytes=VMEM_LIMIT),
        name="move",
    )(*blocks, parts, noise)


def noise_kernel(at_ref, b_ref, o_ref, *, spots, particles, depth, scale):
    block, members = o_ref.shape
    zl, core = at_ref[0], at_ref[1]
    t = lax.broadcasted_iota(jnp.int32, (block, members), 0)
    j = lax.broadcasted_iota(jnp.int32, (block, members), 1)
    column = member(zl, core, t // particles, t % particles)
    chosen = jnp.where(j == column, scale, 0.0)
    k = lax.broadcasted_iota(jnp.int32, (members, members), 0)
    m = lax.broadcasted_iota(jnp.int32, (members, members), 1)
    order = (m // block) % depth
    m_zl = (zl + offset(order) + depth) % depth
    m_core = (core + m // (block * depth)) % 2
    row = member(m_zl, m_core, (m // particles) % spots, m % particles)
    chosen_row = jnp.where(k == row, 1.0, 0.0)
    picked = lax.dot_general(
        chosen, b_ref[...], (((1,), (1,)), ((), ())),
        precision=lax.Precision.HIGHEST, preferred_element_type=jnp.float32,
    )
    o_ref[...] = lax.dot_general(
        picked, chosen_row, (((1,), (0,)), ((), ())),
        precision=lax.Precision.HIGHEST, preferred_element_type=jnp.float32,
    )


def ordered_noise(brownian, at, spots, particles, depth, scale):
    return pl.pallas_call(
        lambda *refs: noise_kernel(
            *refs, spots=spots, particles=particles, depth=depth, scale=scale
        ),
        in_specs=[
            pl.BlockSpec(memory_space=pltpu.SMEM),
            pl.BlockSpec(memory_space=pltpu.VMEM),
        ],
        out_shape=jax.ShapeDtypeStruct((spots * particles, brownian.shape[0]), jnp.float32),
        compiler_params=pltpu.CompilerParams(vmem_limit_bytes=VMEM_LIMIT),
        name="noise",
    )(at, brownian)


def shifted(block, axis, shift):
    count = lax.axis_size(axis)
    return lax.ppermute(block, axis, [(i, (i + shift) % count) for i in range(count)])


def on_device(logperm, source, observed, brownian):
    particles, width, rows, lanes = logperm.shape
    slabs = lax.axis_size("y")
    spots = lax.axis_size(SPREAD_AXES)
    depth = lax.axis_size("zl")
    cores = lax.axis_size("c")
    ensemble = particles * spots * depth * cores
    chunk = width * rows // spots
    cells = width * slabs * rows * lanes

    chunks = jnp.swapaxes(logperm.reshape(particles, spots, chunk, lanes), 0, 1)
    own = lax.all_to_all(chunks, SPREAD_AXES, split_axis=0, concat_axis=0, tiled=True)
    own = own.reshape(spots * particles, chunk * lanes)

    y = lax.axis_index("y")
    fields = jnp.stack([source, observed])
    received = []
    for shift in range(1, slabs):
        mine = lax.dynamic_slice_in_dim(logperm, (y + shift) % slabs, 1, axis=0)
        received.append(shifted(jnp.concatenate([mine, fields], axis=0), "y", shift))

    step_size = ensemble / (4.0 * (cells + 1))
    noise_scale = math.sqrt(2.0 * step_size / ensemble)
    at = jnp.stack([lax.axis_index("zl"), lax.axis_index("c")])
    noise = ordered_noise(brownian, at, spots, particles, depth, noise_scale)
    blocks = [own]
    ahead, back = own, own
    for _ in range(depth // 2 - 1):
        ahead, back = shifted(ahead, "zl", 1), shifted(back, "zl", depth - 1)
        ahead, back, noise = lax.optimization_barrier((ahead, back, noise))
        blocks += [ahead, back]
    half = own.shape[0] // 2
    blocks += [shifted(ahead[:half], "zl", 1), shifted(back[half:], "zl", depth - 1)]
    blocks += [shifted(block, "c", 1) for block in blocks]

    gradient = darcy(y, logperm, source, observed, received, chunk)
    g = lax.all_to_all(gradient, SPREAD_AXES + ("y",), split_axis=0, concat_axis=0, tiled=True)
    g = g.reshape(spots * particles, chunk * lanes)

    part = gram_product(blocks, g, 1024)
    part = part + shifted(part, "zh", 1)
    copies = spots * slabs // 2
    parts = jnp.broadcast_to(part[None], (copies,) + part.shape)
    parts = lax.all_to_all(parts, ("x", "y"), split_axis=0, concat_axis=0, tiled=True)
    moved = move(blocks, parts, noise, step_size / ensemble, 1024)
    moved = moved.reshape(spots, particles, chunk, lanes)
    returned = lax.all_to_all(moved, SPREAD_AXES, split_axis=0, concat_axis=0, tiled=True)
    return jnp.swapaxes(returned, 0, 1).reshape(logperm.shape)


def solution(mesh):
    fine = Mesh(mesh.devices.reshape(4, 4, 2, 2, 4), ("x", "zl", "zh", "c", "y"))
    dom = ("x", "zl", "zh", "c")
    return jax.shard_map(
        on_device,
        mesh=fine,
        in_specs=(P(dom, "y", None, None), P("y", None, None), P("y", None, None), P()),
        out_specs=P(dom, "y", None, None),
        check_vma=False,
    )
```

```python
import math

import jax
import jax.numpy as jnp
from jax import lax
from jax.experimental import pallas as pl
from jax.experimental.pallas import tpu as pltpu
from jax.sharding import Mesh
from jax.sharding import PartitionSpec as P

SWEEPS = 8
MISFIT_WEIGHT = 1000.0
PAD = 8
SPREAD_AXES = ("x", "zh")
VMEM_LIMIT = 16 << 20


def offset(order):
    half = (order + 1) // 2
    return jnp.where(order % 2 == 0, half, -half)


def member(zl, core, spot, particle):
    return (spot // 2) * 64 + (zl * 2 + spot % 2) * 8 + core * 4 + particle


def darcy_kernel(
    y_ref, u_ref, src_ref, obs_ref, r1_ref, r2_ref, r3_ref, g_ref,
    e_s, w0, w1, p_s, inv_s, b_s, a_s, src_s, obs_s,
):
    slabs, width, rows, lanes = u_ref.shape
    layers = slabs * width
    lane = lax.broadcasted_iota(jnp.int32, (rows, lanes), 1)
    first = lane == 0
    last = lane == lanes - 1
    mid = pl.ds(PAD, rows)
    up = pl.ds(PAD - 1, rows)
    down = pl.ds(PAD + 1, rows)

    def before(v, fill):
        return jnp.where(first, fill, pltpu.roll(v, 1, 1))

    def after(v, fill):
        return jnp.where(last, fill, pltpu.roll(v, lanes - 1, 1))

    def neighbors(ref, i, fill):
        core = ref[i + 1, mid, :]
        return (
            (ref[i, mid, :] + ref[i + 2, mid, :])
            + (ref[i + 1, up, :] + ref[i + 1, down, :])
            + (before(core, fill) + after(core, fill))
        )

    for ref, fill in ((e_s, 1.0), (w0, 0.0), (w1, 0.0), (p_s, 0.0)):
        ref[:, :PAD, :] = jnp.full((layers + 2, PAD, lanes), fill, jnp.float32)
        ref[:, PAD + rows :, :] = jnp.full((layers + 2, PAD, lanes), fill, jnp.float32)
        for outside in (0, layers + 1):
            ref[outside, mid, :] = jnp.full((rows, lanes), fill, jnp.float32)

    y = y_ref[0]
    for w in range(width):
        e_s[y * width + w + 1, mid, :] = jnp.exp(0.5 * u_ref[y, w])
        src_s[y * width + w] = src_ref[w]
        obs_s[y * width + w] = obs_ref[w]
    for shift, ref in ((1, r1_ref), (2, r2_ref), (3, r3_ref)):
        slab = lax.rem(y + slabs - shift, slabs)
        for w in range(width):
            e_s[slab * width + w + 1, mid, :] = jnp.exp(0.5 * ref[0, w])
            src_s[slab * width + w] = ref[1, w]
            obs_s[slab * width + w] = ref[2, w]

    for i in range(layers):
        inverse = 1.0 / neighbors(e_s, i, 1.0)
        inv_s[i] = inverse
        b_s[i] = inverse * e_s[i + 1, mid, :]
        start = inverse * src_s[i]
        a_s[i] = start
        w0[i + 1, mid, :] = start

    def sweep(now, new):
        for i in range(layers):
            new[i + 1, mid, :] = a_s[i] + b_s[i] * neighbors(now, i, 0.0)

    def relax():
        def two(_, carry):
            sweep(w0, w1)
            sweep(w1, w0)
            return carry

        lax.fori_loop(0, (SWEEPS - 1) // 2, two, 0)
        sweep(w0, w1)

    relax()
    for i in range(layers):
        pressure = w1[i + 1, mid, :] / e_s[i + 1, mid, :]
        p_s[i + 1, mid, :] = pressure
        start = inv_s[i] * (MISFIT_WEIGHT * (pressure - obs_s[i]))
        a_s[i] = start
        w0[i + 1, mid, :] = start
    relax()
    for i in range(layers):
        w1[i + 1, mid, :] = w1[i + 1, mid, :] / e_s[i + 1, mid, :]

    chunk = g_ref.shape[1]
    per_layer = rows // chunk
    for i in range(layers):
        e = e_s[i + 1, mid, :]
        p = p_s[i + 1, mid, :]
        q = w1[i + 1, mid, :]
        total = None
        for at, where in ((i, mid), (i + 2, mid), (i + 1, up), (i + 1, down)):
            term = e_s[at, where, :] * (p - p_s[at, where, :]) * (q - w1[at, where, :])
            total = term if total is None else total + term
        for shift in (before, after):
            total = total + shift(e, 1.0) * (p - shift(p, 0.0)) * (q - shift(q, 0.0))
        gradient = -0.5 * e * total
        for h in range(per_layer):
            spot = (i % width) * per_layer + h
            g_ref[spot * slabs + i // width] = gradient[h * chunk : (h + 1) * chunk]


def darcy(y, u, source, observed, received, chunk):
    slabs, width, rows, lanes = u.shape
    layers = slabs * width
    padded = pltpu.VMEM((layers + 2, rows + 2 * PAD, lanes), jnp.float32)
    plain = pltpu.VMEM((layers, rows, lanes), jnp.float32)
    whole = pl.BlockSpec(memory_space=pltpu.VMEM)
    return pl.pallas_call(
        darcy_kernel,
        in_specs=[pl.BlockSpec(memory_space=pltpu.SMEM)] + [whole] * 6,
        out_specs=whole,
        out_shape=jax.ShapeDtypeStruct((layers * rows // chunk, chunk, lanes), jnp.float32),
        scratch_shapes=[padded] * 4 + [plain] * 5,
        compiler_params=pltpu.CompilerParams(vmem_limit_bytes=VMEM_LIMIT),
        name="darcy",
    )(y.reshape(1), u, source, observed, *received)


def split(v):
    high = v.astype(jnp.bfloat16)
    low = (v - high.astype(jnp.float32)).astype(jnp.bfloat16)
    return high, low


def columns(refs, start, size):
    return jnp.concatenate([ref[:, start : start + size] for ref in refs], axis=0)


def products(u_refs, own_ref, g_ref, tile):
    block, groups, lanes = g_ref.shape
    rows = sum(ref.shape[0] for ref in u_refs)
    dims = (((1,), (1,)), ((), ()))
    total = jnp.zeros((2 * block, rows), jnp.float32)
    for start in range(0, groups * lanes, tile):
        own = own_ref[:, start : start + tile]
        shift = jnp.sum(own, axis=0, keepdims=True) * (1.0 / block)
        s_high, s_low = split(columns(u_refs, start, tile) - shift)
        g = [g_ref[:, r, :] for r in range(start // lanes, (start + tile) // lanes)]
        pair = jnp.concatenate(split(jnp.concatenate(g, axis=1)), axis=0)
        total = total + lax.dot_general(pair, s_high, dims, preferred_element_type=jnp.float32)
        total = total + lax.dot_general(pair, s_low, dims, preferred_element_type=jnp.float32)
    return total[:block] + total[block:]


def early_kernel(*refs, tile):
    *u_refs, g_ref, o_ref = refs
    o_ref[...] = products(u_refs, u_refs[0], g_ref, tile)


def late_kernel(*refs, tile):
    *u_refs, own_ref, g_ref, early_ref, o_ref = refs
    early = early_ref[...]
    late = products(u_refs, own_ref, g_ref, tile)
    sums = jnp.sum(early, axis=1, keepdims=True) + jnp.sum(late, axis=1, keepdims=True)
    mean = sums * (1.0 / o_ref.shape[1])
    o_ref[:, : early.shape[1]] = early - mean
    o_ref[:, early.shape[1] :] = late - mean


def gram_product(early, late, g, tile):
    whole = pl.BlockSpec(memory_space=pltpu.VMEM)

    def call(name, kernel, inputs, members):
        return pl.pallas_call(
            lambda *refs: kernel(*refs, tile=tile),
            in_specs=[whole] * len(inputs),
            out_specs=whole,
            out_shape=jax.ShapeDtypeStruct((g.shape[0], members), jnp.float32),
            compiler_params=pltpu.CompilerParams(vmem_limit_bytes=VMEM_LIMIT),
            name=name,
        )(*inputs)

    first = sum(b.shape[0] for b in early)
    members = first + sum(b.shape[0] for b in late)
    part = call("gram_early", early_kernel, (*early, g), first)
    return call("gram_late", late_kernel, (*late, early[0], g, part), members)


def move_kernel(*refs, scale, tile):
    *u_refs, parts_ref, noise_ref, o_ref = refs
    block, _, lanes = o_ref.shape
    cells = u_refs[0].shape[1]
    members = noise_ref.shape[1]
    total = parts_ref[0]
    for d in range(1, parts_ref.shape[0]):
        total = total + parts_ref[d]
    pair = jnp.concatenate(split(noise_ref[...] - scale * total), axis=0)
    dims = (((1,), (0,)), ((), ()))
    for start in range(0, cells, tile):
        u = columns(u_refs, start, tile)
        s = u - jnp.sum(u, axis=0, keepdims=True) * (1.0 / members)
        s_high, s_low = split(s)
        out = lax.dot_general(pair, s_high, dims, preferred_element_type=jnp.float32)
        out = out + lax.dot_general(pair, s_low, dims, preferred_element_type=jnp.float32)
        moved = u[:block] + 0.25 * s[:block] + (out[:block] + out[block:])
        for r in range(tile // lanes):
            o_ref[:, start // lanes + r, :] = moved[:, r * lanes : (r + 1) * lanes]


def move(blocks, parts, noise, scale, tile):
    block, cells = blocks[0].shape
    lanes = 128
    whole = pl.BlockSpec(memory_space=pltpu.VMEM)
    return pl.pallas_call(
        lambda *refs: move_kernel(*refs, scale=scale, tile=tile),
        in_specs=[whole] * (len(blocks) + 2),
        out_specs=whole,
        out_shape=jax.ShapeDtypeStruct((block, cells // lanes, lanes), jnp.float32),
        compiler_params=pltpu.CompilerParams(vmem_limit_bytes=VMEM_LIMIT),
        name="move",
    )(*blocks, parts, noise)


def noise_kernel(at_ref, b_ref, o_ref, *, spots, particles, depth, scale):
    block, members = o_ref.shape
    zl, core = at_ref[0], at_ref[1]
    t = lax.broadcasted_iota(jnp.int32, (block, members), 0)
    j = lax.broadcasted_iota(jnp.int32, (block, members), 1)
    column = member(zl, core, t // particles, t % particles)
    chosen = jnp.where(j == column, scale, 0.0)
    k = lax.broadcasted_iota(jnp.int32, (members, members), 0)
    m = lax.broadcasted_iota(jnp.int32, (members, members), 1)
    near = depth - 1
    place = m // block
    order = jnp.where(place < 2 * near, place % near, near)
    m_zl = (zl + offset(order) + depth) % depth
    m_core = (core + jnp.where(place < 2 * near, place // near, place - 2 * near)) % 2
    row = member(m_zl, m_core, (m // particles) % spots, m % particles)
    chosen_row = jnp.where(k == row, 1.0, 0.0)
    picked = lax.dot_general(
        chosen, b_ref[...], (((1,), (1,)), ((), ())),
        precision=lax.Precision.HIGHEST, preferred_element_type=jnp.float32,
    )
    o_ref[...] = lax.dot_general(
        picked, chosen_row, (((1,), (0,)), ((), ())),
        precision=lax.Precision.HIGHEST, preferred_element_type=jnp.float32,
    )


def ordered_noise(brownian, at, spots, particles, depth, scale):
    return pl.pallas_call(
        lambda *refs: noise_kernel(
            *refs, spots=spots, particles=particles, depth=depth, scale=scale
        ),
        in_specs=[
            pl.BlockSpec(memory_space=pltpu.SMEM),
            pl.BlockSpec(memory_space=pltpu.VMEM),
        ],
        out_shape=jax.ShapeDtypeStruct((spots * particles, brownian.shape[0]), jnp.float32),
        compiler_params=pltpu.CompilerParams(vmem_limit_bytes=VMEM_LIMIT),
        name="noise",
    )(at, brownian)


def shifted(block, axis, shift):
    count = lax.axis_size(axis)
    return lax.ppermute(block, axis, [(i, (i + shift) % count) for i in range(count)])


def on_device(logperm, source, observed, brownian):
    particles, width, rows, lanes = logperm.shape
    slabs = lax.axis_size("y")
    spots = lax.axis_size(SPREAD_AXES)
    depth = lax.axis_size("zl")
    cores = lax.axis_size("c")
    ensemble = particles * spots * depth * cores
    chunk = width * rows // spots
    cells = width * slabs * rows * lanes

    chunks = jnp.swapaxes(logperm.reshape(particles, spots, chunk, lanes), 0, 1)
    own = lax.all_to_all(chunks, SPREAD_AXES, split_axis=0, concat_axis=0, tiled=True)
    own = own.reshape(spots * particles, chunk * lanes)

    y = lax.axis_index("y")
    fields = jnp.stack([source, observed])
    received = []
    for shift in range(1, slabs):
        mine = lax.dynamic_slice_in_dim(logperm, (y + shift) % slabs, 1, axis=0)
        received.append(shifted(jnp.concatenate([mine, fields], axis=0), "y", shift))

    step_size = ensemble / (4.0 * (cells + 1))
    noise_scale = math.sqrt(2.0 * step_size / ensemble)
    at = jnp.stack([lax.axis_index("zl"), lax.axis_index("c")])
    noise = ordered_noise(brownian, at, spots, particles, depth, noise_scale)
    blocks = [own]
    ahead, back = own, own
    for _ in range(depth // 2 - 1):
        ahead, back = shifted(ahead, "zl", 1), shifted(back, "zl", depth - 1)
        blocks += [ahead, back]
    half = own.shape[0] // 2
    last = [shifted(ahead[:half], "zl", 1), shifted(back[half:], "zl", depth - 1)]
    blocks += [shifted(block, "c", 1) for block in blocks]
    blocks += last + [shifted(block, "c", 1) for block in last]

    received, noise = lax.optimization_barrier((received, noise))
    gradient = darcy(y, logperm, source, observed, received, chunk)
    g = lax.all_to_all(gradient, SPREAD_AXES + ("y",), split_axis=0, concat_axis=0, tiled=True)

    part = gram_product(blocks[:depth], blocks[depth:], g, 1024)
    part = part + shifted(part, "zh", 1)
    copies = spots * slabs // 2
    parts = jnp.broadcast_to(part[None], (copies,) + part.shape)
    parts = lax.all_to_all(parts, ("x", "y"), split_axis=0, concat_axis=0, tiled=True)
    moved = move(blocks, parts, noise, step_size / ensemble, 1024)
    moved = moved.reshape(spots, particles, chunk, lanes)
    returned = lax.all_to_all(moved, SPREAD_AXES, split_axis=0, concat_axis=0, tiled=True)
    return jnp.swapaxes(returned, 0, 1).reshape(logperm.shape)


def solution(mesh):
    fine = Mesh(mesh.devices.reshape(4, 4, 2, 2, 4), ("x", "zl", "zh", "c", "y"))
    dom = ("x", "zl", "zh", "c")
    return jax.shard_map(
        on_device,
        mesh=fine,
        in_specs=(P(dom, "y", None, None), P("y", None, None), P("y", None, None), P()),
        out_specs=P(dom, "y", None, None),
        check_vma=False,
    )
```

```python
import math

import jax
import jax.numpy as jnp
from jax import lax
from jax.experimental import pallas as pl
from jax.experimental.pallas import tpu as pltpu
from jax.sharding import Mesh
from jax.sharding import PartitionSpec as P

SWEEPS = 8
MISFIT_WEIGHT = 1000.0
PAD = 8
SPREAD_AXES = ("x", "zh")
VMEM_LIMIT = 16 << 20


def offset(order):
    half = (order + 1) // 2
    return jnp.where(order % 2 == 0, half, -half)


def member(zl, core, spot, particle):
    return (spot // 2) * 64 + (zl * 2 + spot % 2) * 8 + core * 4 + particle


def darcy_kernel(
    y_ref, u_ref, src_ref, obs_ref, r1_ref, r2_ref, r3_ref, g_ref,
    e_s, w0, w1, p_s, inv_s, b_s, a_s, src_s, obs_s,
):
    slabs, width, rows, lanes = u_ref.shape
    layers = slabs * width
    lane = lax.broadcasted_iota(jnp.int32, (rows, lanes), 1)
    first = lane == 0
    last = lane == lanes - 1
    mid = pl.ds(PAD, rows)
    up = pl.ds(PAD - 1, rows)
    down = pl.ds(PAD + 1, rows)

    def before(v, fill):
        return jnp.where(first, fill, pltpu.roll(v, 1, 1))

    def after(v, fill):
        return jnp.where(last, fill, pltpu.roll(v, lanes - 1, 1))

    def neighbors(ref, i, fill):
        core = ref[i + 1, mid, :]
        return (
            (ref[i, mid, :] + ref[i + 2, mid, :])
            + (ref[i + 1, up, :] + ref[i + 1, down, :])
            + (before(core, fill) + after(core, fill))
        )

    for ref, fill in ((e_s, 1.0), (w0, 0.0), (w1, 0.0), (p_s, 0.0)):
        ref[:, :PAD, :] = jnp.full((layers + 2, PAD, lanes), fill, jnp.float32)
        ref[:, PAD + rows :, :] = jnp.full((layers + 2, PAD, lanes), fill, jnp.float32)
        for outside in (0, layers + 1):
            ref[outside, mid, :] = jnp.full((rows, lanes), fill, jnp.float32)

    y = y_ref[0]
    for w in range(width):
        e_s[y * width + w + 1, mid, :] = jnp.exp(0.5 * u_ref[y, w])
        src_s[y * width + w] = src_ref[w]
        obs_s[y * width + w] = obs_ref[w]
    for shift, ref in ((1, r1_ref), (2, r2_ref), (3, r3_ref)):
        slab = lax.rem(y + slabs - shift, slabs)
        for w in range(width):
            e_s[slab * width + w + 1, mid, :] = jnp.exp(0.5 * ref[0, w])
            src_s[slab * width + w] = ref[1, w]
            obs_s[slab * width + w] = ref[2, w]

    for i in range(layers):
        inverse = 1.0 / neighbors(e_s, i, 1.0)
        inv_s[i] = inverse
        b_s[i] = inverse * e_s[i + 1, mid, :]
        start = inverse * src_s[i]
        a_s[i] = start
        w0[i + 1, mid, :] = start

    def sweep(now, new):
        for i in range(layers):
            new[i + 1, mid, :] = a_s[i] + b_s[i] * neighbors(now, i, 0.0)

    def relax():
        def two(_, carry):
            sweep(w0, w1)
            sweep(w1, w0)
            return carry

        lax.fori_loop(0, (SWEEPS - 1) // 2, two, 0)
        sweep(w0, w1)

    relax()
    for i in range(layers):
        pressure = w1[i + 1, mid, :] / e_s[i + 1, mid, :]
        p_s[i + 1, mid, :] = pressure
        start = inv_s[i] * (MISFIT_WEIGHT * (pressure - obs_s[i]))
        a_s[i] = start
        w0[i + 1, mid, :] = start
    relax()
    for i in range(layers):
        w1[i + 1, mid, :] = w1[i + 1, mid, :] / e_s[i + 1, mid, :]

    chunk = g_ref.shape[1]
    per_layer = rows // chunk
    for i in range(layers):
        e = e_s[i + 1, mid, :]
        p = p_s[i + 1, mid, :]
        q = w1[i + 1, mid, :]
        total = None
        for at, where in ((i, mid), (i + 2, mid), (i + 1, up), (i + 1, down)):
            term = e_s[at, where, :] * (p - p_s[at, where, :]) * (q - w1[at, where, :])
            total = term if total is None else total + term
        for shift in (before, after):
            total = total + shift(e, 1.0) * (p - shift(p, 0.0)) * (q - shift(q, 0.0))
        gradient = -0.5 * e * total
        for h in range(per_layer):
            spot = (i % width) * per_layer + h
            g_ref[spot * slabs + i // width] = gradient[h * chunk : (h + 1) * chunk]


def darcy(y, u, source, observed, received, chunk):
    slabs, width, rows, lanes = u.shape
    layers = slabs * width
    padded = pltpu.VMEM((layers + 2, rows + 2 * PAD, lanes), jnp.float32)
    plain = pltpu.VMEM((layers, rows, lanes), jnp.float32)
    whole = pl.BlockSpec(memory_space=pltpu.VMEM)
    return pl.pallas_call(
        darcy_kernel,
        in_specs=[pl.BlockSpec(memory_space=pltpu.SMEM)] + [whole] * 6,
        out_specs=whole,
        out_shape=jax.ShapeDtypeStruct((layers * rows // chunk, chunk, lanes), jnp.float32),
        scratch_shapes=[padded] * 4 + [plain] * 5,
        compiler_params=pltpu.CompilerParams(vmem_limit_bytes=VMEM_LIMIT),
        name="darcy",
    )(y.reshape(1), u, source, observed, *received)


def split(v):
    high = v.astype(jnp.bfloat16)
    low = (v - high.astype(jnp.float32)).astype(jnp.bfloat16)
    return high, low


def columns(refs, start, size):
    return jnp.concatenate([ref[:, start : start + size] for ref in refs], axis=0)


def gram_kernel(*refs, tile):
    *u_refs, g_ref, o_ref = refs
    block, groups, lanes = g_ref.shape
    cells = groups * lanes
    members = o_ref.shape[1]
    dims = (((1,), (1,)), ((), ()))
    total = jnp.zeros((2 * block, members), jnp.float32)
    for start in range(0, cells, tile):
        u = columns(u_refs, start, tile)
        s_high, s_low = split(u - jnp.sum(u, axis=0, keepdims=True) * (1.0 / members))
        rows = range(start // lanes, (start + tile) // lanes)
        g = jnp.concatenate([g_ref[:, r, :] for r in rows], axis=1)
        pair = jnp.concatenate(split(g), axis=0)
        total = total + lax.dot_general(pair, s_high, dims, preferred_element_type=jnp.float32)
        total = total + lax.dot_general(pair, s_low, dims, preferred_element_type=jnp.float32)
    o_ref[...] = total[:block] + total[block:]


def gram_product(blocks, g, tile):
    members = sum(b.shape[0] for b in blocks)
    whole = pl.BlockSpec(memory_space=pltpu.VMEM)
    return pl.pallas_call(
        lambda *refs: gram_kernel(*refs, tile=tile),
        in_specs=[whole] * (len(blocks) + 1),
        out_specs=whole,
        out_shape=jax.ShapeDtypeStruct((g.shape[0], members), jnp.float32),
        compiler_params=pltpu.CompilerParams(vmem_limit_bytes=VMEM_LIMIT),
        name="gram",
    )(*blocks, g)


def move_kernel(*refs, scale, tile):
    *u_refs, parts_ref, noise_ref, o_ref = refs
    block, _, lanes = o_ref.shape
    cells = u_refs[0].shape[1]
    members = noise_ref.shape[1]
    total = parts_ref[0]
    for d in range(1, parts_ref.shape[0]):
        total = total + parts_ref[d]
    pair = jnp.concatenate(split(noise_ref[...] - scale * total), axis=0)
    dims = (((1,), (0,)), ((), ()))
    for start in range(0, cells, tile):
        u = columns(u_refs, start, tile)
        s = u - jnp.sum(u, axis=0, keepdims=True) * (1.0 / members)
        s_high, s_low = split(s)
        out = lax.dot_general(pair, s_high, dims, preferred_element_type=jnp.float32)
        out = out + lax.dot_general(pair, s_low, dims, preferred_element_type=jnp.float32)
        moved = u[:block] + 0.25 * s[:block] + (out[:block] + out[block:])
        for r in range(tile // lanes):
            o_ref[:, start // lanes + r, :] = moved[:, r * lanes : (r + 1) * lanes]


def move(blocks, parts, noise, scale, tile):
    block, cells = blocks[0].shape
    lanes = 128
    whole = pl.BlockSpec(memory_space=pltpu.VMEM)
    return pl.pallas_call(
        lambda *refs: move_kernel(*refs, scale=scale, tile=tile),
        in_specs=[whole] * (len(blocks) + 2),
        out_specs=whole,
        out_shape=jax.ShapeDtypeStruct((block, cells // lanes, lanes), jnp.float32),
        compiler_params=pltpu.CompilerParams(vmem_limit_bytes=VMEM_LIMIT),
        name="move",
    )(*blocks, parts, noise)


def noise_kernel(at_ref, b_ref, o_ref, *, spots, particles, depth, scale):
    block, members = o_ref.shape
    zl, core = at_ref[0], at_ref[1]
    t = lax.broadcasted_iota(jnp.int32, (block, members), 0)
    j = lax.broadcasted_iota(jnp.int32, (block, members), 1)
    column = member(zl, core, t // particles, t % particles)
    chosen = jnp.where(j == column, scale, 0.0)
    k = lax.broadcasted_iota(jnp.int32, (members, members), 0)
    m = lax.broadcasted_iota(jnp.int32, (members, members), 1)
    order = (m // block) % depth
    m_zl = (zl + offset(order) + depth) % depth
    m_core = (core + m // (block * depth)) % 2
    row = member(m_zl, m_core, (m // particles) % spots, m % particles)
    chosen_row = jnp.where(k == row, 1.0, 0.0)
    picked = lax.dot_general(
        chosen, b_ref[...], (((1,), (1,)), ((), ())),
        precision=lax.Precision.HIGHEST, preferred_element_type=jnp.float32,
    )
    o_ref[...] = lax.dot_general(
        picked, chosen_row, (((1,), (0,)), ((), ())),
        precision=lax.Precision.HIGHEST, preferred_element_type=jnp.float32,
    )


def ordered_noise(brownian, at, spots, particles, depth, scale):
    return pl.pallas_call(
        lambda *refs: noise_kernel(
            *refs, spots=spots, particles=particles, depth=depth, scale=scale
        ),
        in_specs=[
            pl.BlockSpec(memory_space=pltpu.SMEM),
            pl.BlockSpec(memory_space=pltpu.VMEM),
        ],
        out_shape=jax.ShapeDtypeStruct((spots * particles, brownian.shape[0]), jnp.float32),
        compiler_params=pltpu.CompilerParams(vmem_limit_bytes=VMEM_LIMIT),
        name="noise",
    )(at, brownian)


def shifted(block, axis, shift):
    count = lax.axis_size(axis)
    return lax.ppermute(block, axis, [(i, (i + shift) % count) for i in range(count)])


def on_device(logperm, source, observed, brownian):
    particles, width, rows, lanes = logperm.shape
    slabs = lax.axis_size("y")
    spots = lax.axis_size(SPREAD_AXES)
    depth = lax.axis_size("zl")
    cores = lax.axis_size("c")
    ensemble = particles * spots * depth * cores
    chunk = width * rows // spots
    cells = width * slabs * rows * lanes

    chunks = jnp.swapaxes(logperm.reshape(particles, spots, chunk, lanes), 0, 1)
    own = lax.all_to_all(chunks, SPREAD_AXES, split_axis=0, concat_axis=0, tiled=True)
    own = own.reshape(spots * particles, chunk * lanes)

    y = lax.axis_index("y")
    fields = jnp.stack([source, observed])
    received = []
    for shift in range(1, slabs):
        mine = lax.dynamic_slice_in_dim(logperm, (y + shift) % slabs, 1, axis=0)
        received.append(shifted(jnp.concatenate([mine, fields], axis=0), "y", shift))

    step_size = ensemble / (4.0 * (cells + 1))
    noise_scale = math.sqrt(2.0 * step_size / ensemble)
    at = jnp.stack([lax.axis_index("zl"), lax.axis_index("c")])
    noise = ordered_noise(brownian, at, spots, particles, depth, noise_scale)
    blocks = [own]
    ahead, back = own, own
    for _ in range(depth // 2 - 1):
        ahead, back = shifted(ahead, "zl", 1), shifted(back, "zl", depth - 1)
        blocks += [ahead, back]
    half = own.shape[0] // 2
    blocks += [shifted(ahead[:half], "zl", 1), shifted(back[half:], "zl", depth - 1)]
    blocks += [shifted(block, "c", 1) for block in blocks]

    received, noise = lax.optimization_barrier((received, noise))
    gradient = darcy(y, logperm, source, observed, received, chunk)
    g = lax.all_to_all(gradient, SPREAD_AXES + ("y",), split_axis=0, concat_axis=0, tiled=True)

    part = gram_product(blocks, g, 1024)
    part = part + shifted(part, "zh", 1)
    copies = spots * slabs // 2
    parts = jnp.broadcast_to(part[None], (copies,) + part.shape)
    parts = lax.all_to_all(parts, ("x", "y"), split_axis=0, concat_axis=0, tiled=True)
    moved = move(blocks, parts, noise, step_size / ensemble, 1024)
    moved = moved.reshape(spots, particles, chunk, lanes)
    returned = lax.all_to_all(moved, SPREAD_AXES, split_axis=0, concat_axis=0, tiled=True)
    return jnp.swapaxes(returned, 0, 1).reshape(logperm.shape)


def solution(mesh):
    fine = Mesh(mesh.devices.reshape(4, 4, 2, 2, 4), ("x", "zl", "zh", "c", "y"))
    dom = ("x", "zl", "zh", "c")
    return jax.shard_map(
        on_device,
        mesh=fine,
        in_specs=(P(dom, "y", None, None), P("y", None, None), P("y", None, None), P()),
        out_specs=P(dom, "y", None, None),
        check_vma=False,
    )
```
